32 devices in a mesh: dp: 4 (over y, x), expert: 8 (over z, core).
Axes of the slice: x: 2, y: 2, z: 4, core: 2. Of those that a mesh axis runs over, the one named last changes fastest.
Arguments:
- tokens: bfloat16 [2048, 4096], P(('dp', 'expert')), may hold values from -6 to 6
- grads_out: bfloat16 [2048, 4096], P(('dp', 'expert')), may hold values from -6 to 6
- routes: int32 [2048, 2], P(('dp', 'expert')), may hold values from 0 to 31, all different within a row; in each aligned block of 64 rows (0 to 63, 64 to 127, ...) at most 4 rows name the same one
- route_weights: float32 [2048, 2], P(('dp', 'expert')), may hold values from 0.2 to 1
- depth_filter: float32 [32, 5, 512], P('expert'), may hold values from -2.5 to 2.5
- point_weight: bfloat16 [512, 32, 1024], P('dp', 'expert'), may hold values from -0.25 to 0.25
Outputs:
- mixed: bfloat16 [2048, 4096], P(('dp', 'expert'))
- token_grads: bfloat16 [2048, 4096], P(('dp', 'expert'))
- point_grads: float32 [512, 32, 1024], P('dp', 'expert')
- depth_grads: float32 [32, 5, 512], P('expert')
The draws below stay inside these ranges and needn't reach their ends.
Inputs may be any that keep to these rules, and one draw needn't show every extreme that they name: `routes`: the two experts of a frame differ; among the 64 frames of one device no expert is named more than 4 times.
All inputs are finite; a program needn't handle non-finite values.
Results may differ from the reference program's by a relative error of at most 0.0095.
Values may be sent and summed in bfloat16 or wider, within the bound.
No kernel may reach another device: no remote copies, remote signals or barrier semaphores. Data moves between devices by JAX's collectives and lax.ppermute only.
A program may use at most 64 MiB of HBM per device.

```python
import math
import jax
import jax.numpy as jnp
import numpy as np
from jax import lax

C = 512
F = 8
KERNEL_TAPS = 5
DILATION_STEP = 2
EXPERTS = 32
TOK_DEV = 64
CAP = 4
TOKENS = 2048
N_DP = 4
N_EXPERT = 8


def levels(own_key, dims, cuts, smallest, largest):
    factor_of = 1.0
    for dim, blocks in cuts:
        heights = jax.random.uniform(jax.random.fold_in(jax.random.fold_in(own_key, 6), dim), (blocks,), jnp.float32, smallest / len(cuts), largest / len(cuts))
        factor_of = factor_of * jnp.repeat(jnp.exp(heights), dims[dim] // blocks).reshape((-1,) + (1,) * (len(dims) - 1 - dim))
    return factor_of


def assign_block(own_key, own, number, rows, number_of, top, bound, slope):
    sequence = jax.random.permutation(own_key, number_of)
    heavy_load, ordinary = shares(number_of, rows * top, bound, slope, True), shares(number_of, rows * top, bound, slope, False)
    places = jnp.arange(number_of)

    def named(sizes, turn):
        used = int((sizes > 0).sum())
        fixed = max(1, used // 4)
        shifted = fixed + (places - fixed + turn * (used - fixed)) % max(1, number_of - fixed)
        return jnp.zeros((number_of,), jnp.int32).at[sequence[jnp.where(places < fixed, places, shifted)]].set(jnp.asarray(sizes, jnp.int32))

    sizes = jnp.where(number % 4 == 0, named(heavy_load, number // 4), named(ordinary, number - number // 4 - 1))
    mixed = jax.random.permutation(jax.random.fold_in(own, 3), number_of)
    source_of, receiver = mixed[0:number_of // 2 * 2:2], mixed[1:number_of // 2 * 2:2]
    margin = jnp.minimum(sizes[source_of] - 1, bound - sizes[receiver]) // 2
    margin = jnp.where((source_of == sequence[0]) | (receiver == sequence[0]) | (sizes[receiver] == 0), 0, jnp.maximum(margin, 0))
    shifted = jax.random.randint(jax.random.fold_in(own, 4), (number_of // 2,), 0, 1 << 20) % (margin + 1)
    sizes = sizes.at[source_of].add(-shifted).at[receiver].add(shifted)
    items = jnp.searchsorted(jnp.cumsum(sizes), jnp.arange(rows * top), side="right").astype(jnp.int32)
    table = items.reshape(top, rows).T
    table = table[jax.random.permutation(jax.random.fold_in(own, 1), rows)]
    turn = jax.random.randint(jax.random.fold_in(own, 2), (rows, 1), 0, top)
    return jnp.take_along_axis(table, (jnp.arange(top)[None, :] + turn) % top, axis=1)


def shares(amount, total, limit, lean, full):
    portions = [(1 << 20) // math.isqrt(grade ** lean) + 1 for grade in range(1, amount + 1)]
    largest = limit if full else min(limit, max(-(-total // amount), total * portions[0] // sum(portions)))
    least = 1 if total - largest >= amount - 1 else 0
    holding, surplus = [largest] + [least] * (amount - 1), total - largest - least * (amount - 1)
    while surplus > 0:
        movable = [i for i in range(1, amount) if holding[i] < largest] or [i for i in range(1, amount) if holding[i] < limit]
        pool, budget = sum([portions[i] for i in movable]), surplus
        for i in movable:
            addition = min(limit - holding[i], max(1, budget * portions[i] // pool), surplus)
            holding[i] = holding[i] + addition
            surplus = surplus - addition
    return np.array(holding)


def noise(stream_key, extent, deviation, most, pieces=(), kind=jnp.bfloat16):
    gain = levels(stream_key, extent, pieces, -0.22, 0.18) if pieces else 1.0
    result = jax.random.normal(stream_key, extent, jnp.float32) * deviation * gain
    return jnp.minimum(jnp.maximum(result, -most), most).astype(kind)


def setup_inputs(seed: int = 0) -> dict:
    keys = jax.random.split(jax.random.key(seed), 7)
    tokens = noise(keys[0], (TOKENS, F * C), 1.0, 6.0, ((0, 32),))
    grads_out = noise(keys[1], (TOKENS, F * C), 1.0, 6.0, ((0, 32),))
    routes_keys = jax.random.split(jax.random.fold_in(keys[2], 1), TOKENS // TOK_DEV)
    routes_turns = jax.random.permutation(jax.random.fold_in(keys[2], 3), TOKENS // TOK_DEV)
    routes = jax.vmap(lambda own, number: assign_block(jax.random.fold_in(keys[2], 2), own, number, TOK_DEV, EXPERTS, 2, CAP, 2))(routes_keys, routes_turns).reshape((TOKENS, 2))
    route_weights = jnp.clip(0.2 + 0.8 * jax.random.uniform(keys[3], (TOKENS, 2), jnp.float32) ** levels(keys[3], (TOKENS, 2), ((0, 32),), -0.2, 0.2), 0.2, 1.0)
    depth_filter = noise(keys[4], (EXPERTS, KERNEL_TAPS, C), 0.45, 2.5, ((0, 8),), jnp.float32)
    point_weight = noise(keys[5], (C, EXPERTS, 2 * C), C ** -0.5, 0.25, ((0, 4), (1, 8)))
    return {"tokens": tokens, "grads_out": grads_out, "routes": routes, "route_weights": route_weights, "depth_filter": depth_filter, "point_weight": point_weight}


def shifted_input(field, tap_offset):
    width = field.shape[-2]
    pads = [(0, 0)] * (field.ndim - 2) + [(abs(tap_offset), abs(tap_offset)), (0, 0)]
    padded = jnp.pad(field, pads)
    begin = abs(tap_offset) + tap_offset
    return lax.slice_in_dim(padded, begin, begin + width, axis=field.ndim - 2)


def reference(tokens, grads_out, routes, route_weights, depth_filter, point_weight):
    dev_count = N_DP * N_EXPERT
    slot_count = 2 * TOK_DEV
    route_flat = routes.reshape(dev_count, slot_count)
    weight_flat = route_weights.reshape(dev_count, slot_count)
    onehot = (route_flat[:, :, None] == jnp.arange(EXPERTS, dtype=jnp.int32)[None, None, :]).astype(jnp.int32)
    ranks = jnp.sum((jnp.cumsum(onehot, axis=1) - 1) * onehot, axis=2)
    slot_ids = route_flat * CAP + ranks
    cap_iota = jnp.arange(CAP, dtype=jnp.int32)
    row_iota = jnp.arange(slot_count, dtype=jnp.int32)
    base_rows = jnp.arange(dev_count, dtype=jnp.int32) * TOK_DEV
    bucket_rows = dev_count * CAP

    def expert_step(carry, expert_id):
        mixed_acc, grads_acc = carry
        matched = (slot_ids[:, None, :] == (expert_id * CAP + cap_iota)[None, :, None]).astype(jnp.int32)
        valid = jnp.sum(matched, axis=2).reshape(-1).astype(jnp.float32)
        entry = jnp.sum(matched * row_iota[None, None, :], axis=2)
        frame_idx = (base_rows[:, None] + entry // 2).reshape(-1).astype(jnp.int32)
        slot_weight = jnp.sum(matched.astype(jnp.float32) * weight_flat[:, None, :], axis=2).reshape(-1)
        input_frames = (tokens[frame_idx].astype(jnp.float32) * valid[:, None]).reshape(bucket_rows, F, C)
        cotan = (slot_weight[:, None] * grads_out[frame_idx].astype(jnp.float32)).astype(jnp.bfloat16)
        cotan = cotan.reshape(bucket_rows, F, C).astype(jnp.float32)
        tap_weights = lax.dynamic_index_in_dim(depth_filter, expert_id, 0, keepdims=False)
        matrix = lax.dynamic_index_in_dim(point_weight, expert_id, 1, keepdims=False)
        hidden_state = jnp.zeros((bucket_rows, F, C), jnp.float32)
        for tap_index in range(KERNEL_TAPS):
            hidden_state = hidden_state + tap_weights[tap_index][None, None, :] * shifted_input(input_frames, DILATION_STEP * (tap_index - KERNEL_TAPS // 2))
        hidden_state = hidden_state.astype(jnp.bfloat16)
        preact = jnp.dot(hidden_state.reshape(-1, C), matrix, preferred_element_type=jnp.float32).reshape(bucket_rows, F, 2 * C)
        value_half = preact[..., :C]
        gate_sig = jax.nn.sigmoid(preact[..., C:])
        expert_out = (value_half * gate_sig).astype(jnp.bfloat16)
        dpre = jnp.concatenate([cotan * gate_sig, cotan * value_half * gate_sig * (1.0 - gate_sig)], axis=-1).astype(jnp.bfloat16)
        dhidden = jnp.dot(dpre.reshape(-1, 2 * C), matrix.T, preferred_element_type=jnp.float32).reshape(bucket_rows, F, C)
        frame_grad = jnp.zeros((bucket_rows, F, C), jnp.float32)
        tap_grads = []
        for tap_index in range(KERNEL_TAPS):
            tap_offset = DILATION_STEP * (tap_index - KERNEL_TAPS // 2)
            frame_grad = frame_grad + tap_weights[tap_index][None, None, :] * shifted_input(dhidden, -tap_offset)
            tap_grads.append(jnp.sum(dhidden * shifted_input(input_frames, tap_offset), axis=(0, 1)))
        frame_grad = frame_grad.astype(jnp.bfloat16)
        hidden_rows = hidden_state.reshape(N_DP, N_EXPERT * CAP * F, C).astype(jnp.float32)
        dpre_rows = dpre.reshape(N_DP, N_EXPERT * CAP * F, 2 * C).astype(jnp.float32)
        partial_value = jnp.einsum("nrc,nro->nco", hidden_rows, dpre_rows, precision=lax.Precision.HIGHEST)
        weight_grad = jnp.sum(partial_value.astype(jnp.bfloat16).astype(jnp.float32), axis=0)
        mixed_acc = mixed_acc.at[frame_idx].add(slot_weight[:, None] * expert_out.reshape(bucket_rows, F * C).astype(jnp.float32))
        grads_acc = grads_acc.at[frame_idx].add(frame_grad.reshape(bucket_rows, F * C).astype(jnp.float32))
        return (mixed_acc, grads_acc), (weight_grad, jnp.stack(tap_grads, axis=0))

    start = (jnp.zeros((TOKENS, F * C), jnp.float32), jnp.zeros((TOKENS, F * C), jnp.float32))
    (mixed_acc, grads_acc), (weight_grads, depth_grads) = lax.scan(expert_step, start, jnp.arange(EXPERTS, dtype=jnp.int32))
    point_grads = jnp.transpose(weight_grads, (1, 0, 2))
    return mixed_acc.astype(jnp.bfloat16), grads_acc.astype(jnp.bfloat16), point_grads, depth_grads
```

```python
import functools

import jax
import jax.numpy as jnp
from jax import lax
from jax.experimental import pallas as pl
from jax.experimental.pallas import tpu as pltpu
from jax.sharding import PartitionSpec as P

KERNEL_TAPS = 5
DILATION_STEP = 2
CAP = 4
CHUNK = 2
ROWS = 2 * CHUNK * CAP
PAD = 8
OFFSETS = tuple(DILATION_STEP * (j - KERNEL_TAPS // 2) for j in range(KERNEL_TAPS))
F32 = jnp.float32
BF16 = jnp.bfloat16


def params():
    return pltpu.CompilerParams(vmem_limit_bytes=56 * 1024 * 1024)


def dot(a, b, dims=((1,), (0,))):
    return lax.dot_general(a, b, (dims, ((), ())), preferred_element_type=F32)


def column(row):
    size = row.shape[1]
    diagonal = lax.broadcasted_iota(jnp.int32, (size, size), 0) == lax.broadcasted_iota(
        jnp.int32, (size, size), 1
    )
    return jnp.sum(jnp.where(diagonal, row, jnp.zeros_like(row)), axis=1, keepdims=True)


def dispatch_kernel(devs, chunks, chunk, me_ref, routes_ref, weights_ref, tokens_ref, grads_ref, *refs):
    table_ref, pieces, select_ref = refs[0], refs[1:-1], refs[-1]
    toks, width = tokens_ref.shape
    slots = devs * ROWS
    experts = devs * chunks * CHUNK

    @pl.when(pl.program_id(0) == 0)
    def _():
        me = me_ref[0]
        first = column(routes_ref[0:1, :])
        second = column(routes_ref[1:2, :])
        lane_expert = lax.broadcasted_iota(jnp.int32, (toks, experts), 1)
        hit_first = (first == lane_expert).astype(F32)
        hit_second = (second == lane_expert).astype(F32)
        earlier = (
            lax.broadcasted_iota(jnp.int32, (toks, toks), 1)
            < lax.broadcasted_iota(jnp.int32, (toks, toks), 0)
        ).astype(BF16)
        counts = dot(earlier, (hit_first + hit_second).astype(BF16))
        rank_first = jnp.sum(counts * hit_first, axis=1, keepdims=True).astype(jnp.int32)
        rank_second = jnp.sum(counts * hit_second, axis=1, keepdims=True).astype(jnp.int32)
        slot_first = first * CAP + rank_first
        slot_second = second * CAP + rank_second
        lane = lax.broadcasted_iota(jnp.int32, (1, slots), 1)
        piece = lane // ROWS
        within = lane % ROWS
        far = devs // 2
        relative = jnp.where(piece < far, 2 * piece, 2 * (piece - far) + 1)
        is_frame = within // (CHUNK * CAP) == 0
        wanted = ((me ^ relative) * chunks + chunk) * (CHUNK * CAP) + within % (CHUNK * CAP)
        one = lambda mask: jnp.where(mask, 1.0, 0.0).astype(BF16)
        frame_wanted = jnp.where(is_frame, wanted, -1)
        cotan_wanted = jnp.where(is_frame, -1, wanted)
        frame_first = one(slot_first == frame_wanted)
        frame_second = one(slot_second == frame_wanted)
        cotan_first = one(slot_first == cotan_wanted)
        cotan_second = one(slot_second == cotan_wanted)
        table_ref[0:toks] = frame_first
        table_ref[toks : 2 * toks] = frame_second
        table_ref[2 * toks : 3 * toks] = cotan_first + cotan_second
        select_ref[0:toks] = frame_first + frame_second
        select_ref[toks : 2 * toks] = cotan_first
        select_ref[2 * toks : 3 * toks] = cotan_second

    weight_first = column(weights_ref[0:1, :])
    weight_second = column(weights_ref[1:2, :])
    step = min(512, width)
    for begin in range(0, width, step):
        lanes = slice(begin, begin + step)
        grads = grads_ref[:, lanes].astype(F32)
        stacked = jnp.concatenate(
            [
                tokens_ref[:, lanes],
                (weight_first * grads).astype(BF16),
                (weight_second * grads).astype(BF16),
            ],
            axis=0,
        )
        placed = dot(select_ref[...], stacked, ((0,), (0,)))
        begin_row = 0
        for ref in pieces:
            rows = ref.shape[0]
            ref[:, lanes] = placed[begin_row : begin_row + rows].astype(BF16)
            begin_row += rows


def sorting(devs, side):
    total = devs * ROWS
    block = devs * CAP
    row = lax.broadcasted_iota(jnp.int32, (total, total), side)
    expert = row // (2 * block)
    tensor = (row // block) % 2
    device = (row // CAP) % devs
    source = device * ROWS + (tensor * CHUNK + expert) * CAP + row % CAP
    other = lax.broadcasted_iota(jnp.int32, (total, total), 1 - side)
    return jnp.where(source == other, 1.0, 0.0).astype(BF16)


def bits_of(size, expert):
    bits = [1 << k for k in range(size.bit_length() - 1)]
    return bits if expert % 2 == 0 else bits[::-1]


def halving(size, expert):
    rounds, held = [], list(range(size))
    for bit in bits_of(size, expert):
        rounds.append(([r for r in held if r & bit], [r for r in held if not r & bit]))
        held = rounds[-1][1]
    return rounds


def chunk_kernel(devs, held, chunk, *refs):
    me_ref, filter_ref = refs[0], refs[1]
    refs = refs[2:]
    far = devs // 2
    (own_ref, swapped_ref, *far_refs), refs = refs[: far + 1], refs[far + 1 :]
    weight_refs, refs = refs[: len(held)], refs[len(held) :]
    backs, refs = refs[:far], refs[far:]
    reduce_refs, refs = refs[: 2 * CHUNK], refs[2 * CHUNK :]
    matrix, rows_f32, hidden, preact, dpre, dhidden, grad, results = refs
    shards_n = sum(map(len, held)) // CHUNK
    width = own_ref.shape[1]
    channels = matrix.shape[1]
    bins = width // channels
    block = devs * CAP
    total = devs * ROWS
    local = channels // shards_n
    for ref, blocks in zip(weight_refs, held):
        for index, (expert, place, relative) in enumerate(blocks):
            begin = pl.multiple_of((me_ref[0] ^ place if relative else place) * local, local)
            matrix[expert, pl.ds(begin, local), :] = ref[index * local : (index + 1) * local]

    sort = sorting(devs, 0)
    for p in range(bins):
        lanes = slice(p * channels, (p + 1) * channels)
        stacked = [ref[:, lanes] for ref in (own_ref, swapped_ref, *far_refs)]
        rows_f32[:, lanes] = dot(sort, jnp.concatenate(stacked, axis=0))

    for expert in range(CHUNK):
        frames = slice(expert * 2 * block, expert * 2 * block + block)
        cotans = slice(expert * 2 * block + block, (expert + 1) * 2 * block)
        taps = [filter_ref[chunk * CHUNK + expert, j : j + 1, :] for j in range(KERNEL_TAPS)]
        bin_lanes = lambda p: slice(p * channels, (p + 1) * channels)
        bin_rows = lambda p: slice(p * block, (p + 1) * block)
        for p in range(bins):
            acc = None
            for j, off in enumerate(OFFSETS):
                if 0 <= p + off < bins:
                    term = taps[j] * rows_f32[frames, bin_lanes(p + off)]
                    acc = term if acc is None else acc + term
            hidden[bin_rows(p), :] = acc.astype(BF16)
        preact[...] = dot(hidden[...], matrix[expert])
        for p in range(bins):
            value = preact[bin_rows(p), 0:channels]
            sig = 1.0 / (1.0 + jnp.exp(-preact[bin_rows(p), channels : 2 * channels]))
            cotan = rows_f32[cotans, bin_lanes(p)]
            results[frames, bin_lanes(p)] = (value * sig).astype(BF16)
            dpre[bin_rows(p), 0:channels] = (cotan * sig).astype(BF16)
            dpre[bin_rows(p), channels : 2 * channels] = (
                cotan * value * sig * (1.0 - sig)
            ).astype(BF16)
        dhidden[...] = dot(dpre[...], matrix[expert], ((1,), (1,)))
        grad[...] = dot(hidden[...], dpre[...], ((0,), (0,))).astype(BF16)
        rounds = halving(shards_n, expert)[0]
        for ref, relatives in zip(reduce_refs[2 * expert : 2 * expert + 2], rounds):
            for index, relative in enumerate(relatives):
                begin = pl.multiple_of((me_ref[0] ^ relative) * local, local)
                row = index * (local + PAD)
                ref[row : row + local, :] = grad[pl.ds(begin, local), :]
        for q in range(bins):
            acc = None
            for j, off in enumerate(OFFSETS):
                if 0 <= q - off < bins:
                    term = taps[j] * dhidden[bin_rows(q - off), :]
                    acc = term if acc is None else acc + term
            results[cotans, bin_lanes(q)] = acc.astype(BF16)
        lines = []
        for j, off in enumerate(OFFSETS):
            acc = None
            for p in range(bins):
                if 0 <= p + off < bins:
                    term = dhidden[bin_rows(p), :] * rows_f32[frames, bin_lanes(p + off)]
                    acc = term if acc is None else acc + term
            lines.append(jnp.sum(acc, axis=0, keepdims=True))
        tail = jnp.concatenate(lines + [jnp.zeros((PAD - KERNEL_TAPS, channels), F32)], axis=0)
        tail = jnp.concatenate([tail, jnp.zeros_like(tail)], axis=1).astype(BF16)
        for ref in reduce_refs[2 * expert : 2 * expert + 2]:
            for row in range(local, ref.shape[0], local + PAD):
                ref[row : row + PAD, :] = tail
    unsort = sorting(devs, 1)
    for p in range(bins):
        lanes = slice(p * channels, (p + 1) * channels)
        placed = dot(unsort, results[:, lanes])
        for r, ref in enumerate(backs):
            ref[:, lanes] = placed[2 * r * ROWS : 2 * (r + 1) * ROWS].astype(BF16)


def combine_kernel(chunks, weights_ref, *refs):
    tables, pieces, (mixed_ref, grads_ref) = refs[:chunks], refs[chunks:-2], refs[-2:]
    each = len(pieces) // chunks
    toks, width = mixed_ref.shape
    weight_first = column(weights_ref[0:1, :])
    weight_second = column(weights_ref[1:2, :])
    step = min(512, width)
    for begin in range(0, width, step):
        lanes = slice(begin, begin + step)
        placed = None
        for index, table_ref in enumerate(tables):
            stacked = [ref[:, lanes] for ref in pieces[index * each : (index + 1) * each]]
            part = dot(table_ref[...], jnp.concatenate(stacked, axis=0))
            placed = part if placed is None else placed + part
        mixed_ref[:, lanes] = (
            weight_first * placed[0:toks] + weight_second * placed[toks : 2 * toks]
        ).astype(BF16)
        grads_ref[:, lanes] = placed[2 * toks : 3 * toks].astype(BF16)


VMEM = pl.BlockSpec(memory_space=pltpu.VMEM)
SMEM = pl.BlockSpec(memory_space=pltpu.SMEM)
COSTS = (2, 3, 2)
LATE = False
PLANE = 4
WINDOW = 3


def cost(work):
    return pl.CostEstimate(flops=work * 10**9, transcendentals=0, bytes_accessed=8 * 1024 * 1024)


def flip(value, axis, bits):
    return lax.ppermute(value, axis, [(k, k ^ bits) for k in range(lax.axis_size(axis))])


def after(value, *others):
    return lax.optimization_barrier((value, *others))[0]


def shards(tokens, grads_out, routes, route_weights, depth_filter, point_weight):
    toks, width = tokens.shape
    devs = lax.axis_size("expert")
    shards_n = lax.axis_size("dp")
    exp_local = depth_filter.shape[0]
    chunks = exp_local // CHUNK
    local, _, out_channels = point_weight.shape
    channels = local * shards_n
    bins = width // channels
    block = devs * CAP
    total = devs * ROWS
    far = devs // 2
    order = sorted(range(1, far), reverse=True)
    me = lax.axis_index("expert").astype(jnp.int32).reshape(1)
    me_dp = lax.axis_index("dp").astype(jnp.int32).reshape(1)
    routes = routes.T
    route_weights = route_weights.T

    whole = lambda *shape: pl.BlockSpec(shape, lambda i: (0,) * len(shape))
    piece = jax.ShapeDtypeStruct((ROWS, width), BF16)
    tables, sent = [], []
    for chunk in range(chunks):
        table, *pieces = pl.pallas_call(
            functools.partial(dispatch_kernel, devs, chunks, chunk),
            grid=(1,),
            out_shape=[jax.ShapeDtypeStruct((3 * toks, total), BF16)]
            + [piece] * far
            + [jax.ShapeDtypeStruct((far * ROWS, width), BF16)],
            in_specs=[SMEM, whole(2, toks), whole(2, toks), whole(toks, width), whole(toks, width)],
            out_specs=[whole(3 * toks, total)]
            + [whole(ROWS, width)] * far
            + [whole(far * ROWS, width)],
            scratch_shapes=[pltpu.VMEM((3 * toks, total), BF16)],
            compiler_params=params(),
            cost_estimate=cost(COSTS[0]),
            name="dispatch",
        )(me, routes, route_weights, tokens, grads_out)
        tables.append(table)
        sent.append(pieces)

    line = []

    def along_line(pieces):
        moved = {0: pieces[0]}
        for r in order:
            value = pieces[r]
            if len(line) >= WINDOW:
                value = after(value, line[-WINDOW])
            line.append(flip(value, "expert", 2 * r))
            moved[r] = line[-1]
        return [moved[r] for r in range(far)]

    plane = []

    def in_plane(value, bit):
        if len(plane) >= PLANE:
            value = after(value, plane[-PLANE])
        plane.append(flip(value, "dp", bit))
        return plane[-1]

    def gather(parts):
        held = [(part, [0]) for part in parts]
        for turn in range(shards_n.bit_length() - 1):
            bits = [bits_of(shards_n, expert)[turn] for expert in range(CHUNK)]
            came = [in_plane(value, bit) for (value, _), bit in zip(held, bits)]
            new = [
                (other, [place ^ bit for place in places])
                for (_, places), other, bit in zip(held, came, bits)
            ]
            if 2 * len(held[0][1]) == shards_n:
                return [
                    (value, [(expert, place, True) for place in places])
                    for expert in range(CHUNK)
                    for value, places in (held[expert], new[expert])
                ]
            held = [
                (jnp.concatenate([old, other], axis=0), places + more)
                for (old, places), (other, more) in zip(held, new)
            ]

    def scatter(pairs):
        rounds = [halving(shards_n, expert) for expert in range(CHUNK)]
        size = local + PAD
        for turn in range(len(rounds[0])):
            came = [
                in_plane(send, bits_of(shards_n, expert)[turn])
                for expert, (send, _) in enumerate(pairs)
            ]
            if turn + 1 == len(rounds[0]):
                return [
                    keep.astype(F32) + other.astype(F32)
                    for (_, keep), other in zip(pairs, came)
                ]
            new = []
            for expert, ((_, keep), other) in enumerate(zip(pairs, came)):
                places = rounds[expert][turn][1]
                total = lambda r: (
                    keep[places.index(r) * size : (places.index(r) + 1) * size].astype(F32)
                    + other[places.index(r) * size : (places.index(r) + 1) * size].astype(F32)
                ).astype(BF16)
                new.append(
                    [
                        jnp.concatenate([total(r) for r in relatives], axis=0)
                        for relatives in rounds[expert][turn + 1]
                    ]
                )
            pairs = new

    weights = jnp.transpose(after(point_weight, tables[0]), (1, 0, 2))
    arrived = []
    for *own, relayed in sent:
        relayed = flip(relayed, "expert", 1)
        pairs = [
            jnp.concatenate([own[r], relayed[r * ROWS : (r + 1) * ROWS]], axis=0)
            for r in range(1, far)
        ]
        arrived.append([own[0], relayed] + along_line([own[0]] + pairs)[1:])
    gathered = [
        gather(
            [
                after(weights[chunk * CHUNK + expert], arrived[chunk][1])
                for expert in range(CHUNK)
            ]
        )
        for chunk in range(chunks)
    ]
    half = jax.ShapeDtypeStruct((shards_n // 2 * (local + PAD), out_channels), BF16)
    backs = []
    reduced = []
    for chunk in range(chunks):
        full, held = zip(*gathered[chunk])
        pair = jax.ShapeDtypeStruct((2 * ROWS, width), BF16)
        outs = [pair] * far + [half] * (2 * CHUNK)
        outs = pl.pallas_call(
            functools.partial(chunk_kernel, devs, held, chunk),
            out_shape=outs,
            grid=(1,),
            in_specs=[SMEM, whole(*depth_filter.shape)]
            + [whole(ROWS, width)] * 2
            + [whole(*value.shape) for value in (*arrived[chunk][2:], *full)],
            out_specs=[whole(*value.shape) for value in outs],
            scratch_shapes=[
                pltpu.VMEM((CHUNK, channels, out_channels), BF16),
                pltpu.VMEM((total, width), F32),
                pltpu.VMEM((bins * block, channels), BF16),
                pltpu.VMEM((bins * block, out_channels), F32),
                pltpu.VMEM((bins * block, out_channels), BF16),
                pltpu.VMEM((bins * block, channels), F32),
                pltpu.VMEM((channels, out_channels), BF16),
                pltpu.VMEM((total, width), BF16),
            ],
            compiler_params=params(),
            cost_estimate=cost(COSTS[1]),
            name="experts",
        )(me_dp, depth_filter, *arrived[chunk], *full)
        results, to_reduce = list(outs[:far]), outs[far:]
        reduced += scatter(list(zip(to_reduce[::2], to_reduce[1::2])))
        if LATE and chunk + 1 == chunks:
            results[1] = after(results[1], *reduced)
        near = along_line(results)
        swapped = flip(jnp.concatenate([value[ROWS:] for value in near], axis=0), "expert", 1)
        backs += near + [swapped]

    mixed, token_grads = pl.pallas_call(
        functools.partial(combine_kernel, chunks),
        grid=(1,),
        out_shape=[jax.ShapeDtypeStruct((toks, width), BF16)] * 2,
        in_specs=[whole(2, toks)]
        + [whole(3 * toks, total)] * chunks
        + ([whole(ROWS, width)] * far + [whole(far * ROWS, width)]) * chunks,
        out_specs=[whole(toks, width)] * 2,
        compiler_params=params(),
        cost_estimate=cost(COSTS[2]),
        name="combine",
    )(route_weights, *tables, *backs)
    point_grads = jnp.stack([value[:local] for value in reduced], axis=1)
    depth_grads = jnp.stack(
        [value[local : local + KERNEL_TAPS, :channels] for value in reduced], axis=0
    )
    return (mixed, token_grads, point_grads, depth_grads)


def solution(mesh):
    placed = (
        P(("dp", "expert"), None),
        P(("dp", "expert"), None),
        P(("dp", "expert"), None),
        P(("dp", "expert"), None),
        P("expert", None, None),
        P("dp", "expert", None),
    )
    return jax.shard_map(
        shards,
        mesh=mesh,
        in_specs=placed,
        out_specs=(
            P(("dp", "expert"), None),
            P(("dp", "expert"), None),
            P("dp", "expert", None),
            P("expert", None, None),
        ),
        check_vma=False,
    )
```

```python
import functools

import jax
import jax.numpy as jnp
from jax import lax
from jax.experimental import pallas as pl
from jax.experimental.pallas import tpu as pltpu
from jax.sharding import PartitionSpec as P

KERNEL_TAPS = 5
DILATION_STEP = 2
CAP = 4
CHUNK = 2
ROWS = 2 * CHUNK * CAP
PAD = 8
OFFSETS = tuple(DILATION_STEP * (j - KERNEL_TAPS // 2) for j in range(KERNEL_TAPS))
F32 = jnp.float32
BF16 = jnp.bfloat16


def params():
    return pltpu.CompilerParams(vmem_limit_bytes=56 * 1024 * 1024)


def dot(a, b, dims=((1,), (0,))):
    return lax.dot_general(a, b, (dims, ((), ())), preferred_element_type=F32)


def column(row):
    size = row.shape[1]
    diagonal = lax.broadcasted_iota(jnp.int32, (size, size), 0) == lax.broadcasted_iota(
        jnp.int32, (size, size), 1
    )
    return jnp.sum(jnp.where(diagonal, row, jnp.zeros_like(row)), axis=1, keepdims=True)


def dispatch_kernel(devs, chunks, chunk, me_ref, routes_ref, weights_ref, tokens_ref, grads_ref, *refs):
    table_ref, pieces, select_ref = refs[0], refs[1:-1], refs[-1]
    toks, width = tokens_ref.shape
    slots = devs * ROWS
    experts = devs * chunks * CHUNK

    @pl.when(pl.program_id(0) == 0)
    def _():
        me = me_ref[0]
        first = column(routes_ref[0:1, :])
        second = column(routes_ref[1:2, :])
        lane_expert = lax.broadcasted_iota(jnp.int32, (toks, experts), 1)
        hit_first = (first == lane_expert).astype(F32)
        hit_second = (second == lane_expert).astype(F32)
        earlier = (
            lax.broadcasted_iota(jnp.int32, (toks, toks), 1)
            < lax.broadcasted_iota(jnp.int32, (toks, toks), 0)
        ).astype(BF16)
        counts = dot(earlier, (hit_first + hit_second).astype(BF16))
        rank_first = jnp.sum(counts * hit_first, axis=1, keepdims=True).astype(jnp.int32)
        rank_second = jnp.sum(counts * hit_second, axis=1, keepdims=True).astype(jnp.int32)
        slot_first = first * CAP + rank_first
        slot_second = second * CAP + rank_second
        lane = lax.broadcasted_iota(jnp.int32, (1, slots), 1)
        piece = lane // ROWS
        within = lane % ROWS
        far = devs // 2
        relative = jnp.where(piece < far, 2 * piece, 2 * (piece - far) + 1)
        is_frame = within // (CHUNK * CAP) == 0
        wanted = ((me ^ relative) * chunks + chunk) * (CHUNK * CAP) + within % (CHUNK * CAP)
        one = lambda mask: jnp.where(mask, 1.0, 0.0).astype(BF16)
        frame_wanted = jnp.where(is_frame, wanted, -1)
        cotan_wanted = jnp.where(is_frame, -1, wanted)
        frame_first = one(slot_first == frame_wanted)
        frame_second = one(slot_second == frame_wanted)
        cotan_first = one(slot_first == cotan_wanted)
        cotan_second = one(slot_second == cotan_wanted)
        table_ref[0:toks] = frame_first
        table_ref[toks : 2 * toks] = frame_second
        table_ref[2 * toks : 3 * toks] = cotan_first + cotan_second
        select_ref[0:toks] = frame_first + frame_second
        select_ref[toks : 2 * toks] = cotan_first
        select_ref[2 * toks : 3 * toks] = cotan_second

    weight_first = column(weights_ref[0:1, :])
    weight_second = column(weights_ref[1:2, :])
    step = min(512, width)
    for begin in range(0, width, step):
        lanes = slice(begin, begin + step)
        grads = grads_ref[:, lanes].astype(F32)
        stacked = jnp.concatenate(
            [
                tokens_ref[:, lanes],
                (weight_first * grads).astype(BF16),
                (weight_second * grads).astype(BF16),
            ],
            axis=0,
        )
        placed = dot(select_ref[...], stacked, ((0,), (0,)))
        begin_row = 0
        for ref in pieces:
            rows = ref.shape[0]
            ref[:, lanes] = placed[begin_row : begin_row + rows].astype(BF16)
            begin_row += rows


def sorting(devs, side):
    total = devs * ROWS
    block = devs * CAP
    row = lax.broadcasted_iota(jnp.int32, (total, total), side)
    expert = row // (2 * block)
    tensor = (row // block) % 2
    device = (row // CAP) % devs
    source = device * ROWS + (tensor * CHUNK + expert) * CAP + row % CAP
    other = lax.broadcasted_iota(jnp.int32, (total, total), 1 - side)
    return jnp.where(source == other, 1.0, 0.0).astype(BF16)


def bits_of(size, expert):
    bits = [1 << k for k in range(size.bit_length() - 1)]
    return bits if expert % 2 == 0 else bits[::-1]


def chunk_kernel(devs, held, chunk, *refs):
    me_ref, filter_ref = refs[0], refs[1]
    refs = refs[2:]
    far = devs // 2
    (own_ref, swapped_ref, *far_refs), refs = refs[: far + 1], refs[far + 1 :]
    weight_refs, refs = refs[: len(held)], refs[len(held) :]
    backs, refs = refs[:far], refs[far:]
    shards_n = sum(map(len, held)) // CHUNK
    reduce_refs, refs = refs[:shards_n], refs[shards_n:]
    matrix, rows_f32, hidden, preact, dpre, dhidden, grad, results = refs
    width = own_ref.shape[1]
    channels = matrix.shape[1]
    bins = width // channels
    block = devs * CAP
    total = devs * ROWS
    local = channels // shards_n
    for ref, blocks in zip(weight_refs, held):
        for index, (expert, place, relative) in enumerate(blocks):
            begin = pl.multiple_of((me_ref[0] ^ place if relative else place) * local, local)
            matrix[expert, pl.ds(begin, local), :] = ref[index * local : (index + 1) * local]

    sort = sorting(devs, 0)
    for p in range(bins):
        lanes = slice(p * channels, (p + 1) * channels)
        stacked = [ref[:, lanes] for ref in (own_ref, swapped_ref, *far_refs)]
        rows_f32[:, lanes] = dot(sort, jnp.concatenate(stacked, axis=0))

    for expert in range(CHUNK):
        frames = slice(expert * 2 * block, expert * 2 * block + block)
        cotans = slice(expert * 2 * block + block, (expert + 1) * 2 * block)
        taps = [filter_ref[chunk * CHUNK + expert, j : j + 1, :] for j in range(KERNEL_TAPS)]
        bin_lanes = lambda p: slice(p * channels, (p + 1) * channels)
        bin_rows = lambda p: slice(p * block, (p + 1) * block)
        for p in range(bins):
            acc = None
            for j, off in enumerate(OFFSETS):
                if 0 <= p + off < bins:
                    term = taps[j] * rows_f32[frames, bin_lanes(p + off)]
                    acc = term if acc is None else acc + term
            hidden[bin_rows(p), :] = acc.astype(BF16)
        preact[...] = dot(hidden[...], matrix[expert])
        for p in range(bins):
            value = preact[bin_rows(p), 0:channels]
            sig = 1.0 / (1.0 + jnp.exp(-preact[bin_rows(p), channels : 2 * channels]))
            cotan = rows_f32[cotans, bin_lanes(p)]
            results[frames, bin_lanes(p)] = (value * sig).astype(BF16)
            dpre[bin_rows(p), 0:channels] = (cotan * sig).astype(BF16)
            dpre[bin_rows(p), channels : 2 * channels] = (
                cotan * value * sig * (1.0 - sig)
            ).astype(BF16)
        dhidden[...] = dot(dpre[...], matrix[expert], ((1,), (1,)))
        grad[...] = dot(hidden[...], dpre[...], ((0,), (0,))).astype(BF16)
        for relative, ref in enumerate(reduce_refs):
            begin = pl.multiple_of((me_ref[0] ^ relative) * local, local)
            ref[expert * local : (expert + 1) * local, :] = grad[pl.ds(begin, local), :]
        for q in range(bins):
            acc = None
            for j, off in enumerate(OFFSETS):
                if 0 <= q - off < bins:
                    term = taps[j] * dhidden[bin_rows(q - off), :]
                    acc = term if acc is None else acc + term
            results[cotans, bin_lanes(q)] = acc.astype(BF16)
        lines = []
        for j, off in enumerate(OFFSETS):
            acc = None
            for p in range(bins):
                if 0 <= p + off < bins:
                    term = dhidden[bin_rows(p), :] * rows_f32[frames, bin_lanes(p + off)]
                    acc = term if acc is None else acc + term
            lines.append(jnp.sum(acc, axis=0, keepdims=True))
        tail = jnp.concatenate(lines + [jnp.zeros((PAD - KERNEL_TAPS, channels), F32)], axis=0)
        lanes = slice(expert * channels, (expert + 1) * channels)
        for ref in reduce_refs:
            ref[CHUNK * local : CHUNK * local + PAD, lanes] = tail.astype(BF16)
    unsort = sorting(devs, 1)
    for p in range(bins):
        lanes = slice(p * channels, (p + 1) * channels)
        placed = dot(unsort, results[:, lanes])
        for r, ref in enumerate(backs):
            ref[:, lanes] = placed[2 * r * ROWS : 2 * (r + 1) * ROWS].astype(BF16)


def combine_kernel(chunks, weights_ref, *refs):
    tables, pieces, (mixed_ref, grads_ref) = refs[:chunks], refs[chunks:-2], refs[-2:]
    each = len(pieces) // chunks
    toks, width = mixed_ref.shape
    weight_first = column(weights_ref[0:1, :])
    weight_second = column(weights_ref[1:2, :])
    step = min(512, width)
    for begin in range(0, width, step):
        lanes = slice(begin, begin + step)
        placed = None
        for index, table_ref in enumerate(tables):
            stacked = [ref[:, lanes] for ref in pieces[index * each : (index + 1) * each]]
            part = dot(table_ref[...], jnp.concatenate(stacked, axis=0))
            placed = part if placed is None else placed + part
        mixed_ref[:, lanes] = (
            weight_first * placed[0:toks] + weight_second * placed[toks : 2 * toks]
        ).astype(BF16)
        grads_ref[:, lanes] = placed[2 * toks : 3 * toks].astype(BF16)


VMEM = pl.BlockSpec(memory_space=pltpu.VMEM)
SMEM = pl.BlockSpec(memory_space=pltpu.SMEM)
COSTS = (2, 3, 2)
LATE = 1
PLANE = 2
AG1_FIRST = True
D1_AFTER = "gather0last"
K_AFTER = ["gather1first", ""]
R_AFTER = ['gather1last', 'sums0']
R_LAST = ["", ""]
WINDOW = 3


def cost(work):
    return pl.CostEstimate(flops=work * 10**9, transcendentals=0, bytes_accessed=8 * 1024 * 1024)


def flip(value, axis, bits):
    return lax.ppermute(value, axis, [(k, k ^ bits) for k in range(lax.axis_size(axis))])


def after(value, *others):
    return lax.optimization_barrier((value, *others))[0]


def shards(tokens, grads_out, routes, route_weights, depth_filter, point_weight):
    toks, width = tokens.shape
    devs = lax.axis_size("expert")
    shards_n = lax.axis_size("dp")
    exp_local = depth_filter.shape[0]
    chunks = exp_local // CHUNK
    local, _, out_channels = point_weight.shape
    channels = local * shards_n
    bins = width // channels
    block = devs * CAP
    total = devs * ROWS
    far = devs // 2
    order = sorted(range(1, far), reverse=True)
    me = lax.axis_index("expert").astype(jnp.int32).reshape(1)
    me_dp = lax.axis_index("dp").astype(jnp.int32).reshape(1)
    routes = routes.T
    route_weights = route_weights.T

    whole = lambda *shape: pl.BlockSpec(shape, lambda i: (0,) * len(shape))
    piece = jax.ShapeDtypeStruct((ROWS, width), BF16)
    tables, sent = [], []
    for chunk in range(chunks):
        table, *pieces = pl.pallas_call(
            functools.partial(dispatch_kernel, devs, chunks, chunk),
            grid=(1,),
            out_shape=[jax.ShapeDtypeStruct((3 * toks, total), BF16)]
            + [piece] * far
            + [jax.ShapeDtypeStruct((far * ROWS, width), BF16)],
            in_specs=[SMEM, whole(2, toks), whole(2, toks), whole(toks, width), whole(toks, width)],
            out_specs=[whole(3 * toks, total)]
            + [whole(ROWS, width)] * far
            + [whole(far * ROWS, width)],
            scratch_shapes=[pltpu.VMEM((3 * toks, total), BF16)],
            compiler_params=params(),
            cost_estimate=cost(COSTS[0]),
            name="dispatch",
        )(me, routes, route_weights, tokens, grads_out)
        tables.append(table)
        sent.append(pieces)

    line = []

    def along_line(pieces):
        moved = {0: pieces[0]}
        for r in order:
            value = pieces[r]
            if len(line) >= WINDOW:
                value = after(value, line[-WINDOW])
            line.append(flip(value, "expert", 2 * r))
            moved[r] = line[-1]
        return [moved[r] for r in range(far)]

    plane = []
    steps = {}
    rounds_n = shards_n.bit_length() - 1

    def in_plane(value, bit, step):
        if len(plane) >= PLANE:
            value = after(value, plane[-PLANE])
        plane.append(flip(value, "dp", bit))
        steps.setdefault(step, []).append(plane[-1])
        return plane[-1]

    def wait(value, name):
        names = [n for n in (name or "").split() if n]
        others = [v for n in names for v in steps[n]]
        return after(value, *others) if others else value

    def gather(parts, chunk):
        held = [(part, [0]) for part in parts]
        for turn in range(shards_n.bit_length() - 1):
            bits = [bits_of(shards_n, expert)[turn] for expert in range(CHUNK)]
            step = f"gather{chunk}" + ("first" if turn == 0 else "last")
            came = [in_plane(value, bit, step) for (value, _), bit in zip(held, bits)]
            new = [
                (other, [place ^ bit for place in places])
                for (_, places), other, bit in zip(held, came, bits)
            ]
            if 2 * len(held[0][1]) == shards_n:
                return [
                    (value, [(expert, place, True) for place in places])
                    for expert in range(CHUNK)
                    for value, places in (held[expert], new[expert])
                ]
            held = [
                (jnp.concatenate([old, other], axis=0), places + more)
                for (old, places), (other, more) in zip(held, new)
            ]

    weights = jnp.transpose(after(point_weight, tables[0]), (1, 0, 2))
    def dispatched(chunk):
        *own, relayed = sent[chunk]
        relayed = flip(relayed, "expert", 1)
        pairs = [
            jnp.concatenate([own[r], relayed[r * ROWS : (r + 1) * ROWS]], axis=0)
            for r in range(1, far)
        ]
        if chunk > 0:
            pairs = [wait(value, D1_AFTER) for value in pairs]
        return [own[0], relayed] + along_line([own[0]] + pairs)[1:]

    def weights_of(chunk, other):
        parts = [weights[chunk * CHUNK + expert] for expert in range(CHUNK)]
        return gather([after(part, other) for part in parts], chunk)

    arrived = [dispatched(0)]
    gathered = [weights_of(0, arrived[0][1])]
    for chunk in range(1, chunks):
        if AG1_FIRST:
            gathered.append(weights_of(chunk, sent[chunk][-1]))
            arrived.append(dispatched(chunk))
        else:
            arrived.append(dispatched(chunk))
            gathered.append(weights_of(chunk, arrived[chunk][1]))
    block_sum = jax.ShapeDtypeStruct((CHUNK * local + PAD, out_channels), BF16)
    backs = []
    reduced = []
    for chunk in range(chunks):
        full, held = zip(*gathered[chunk])
        arrived[chunk][0] = wait(arrived[chunk][0], K_AFTER[chunk])
        pair = jax.ShapeDtypeStruct((2 * ROWS, width), BF16)
        outs = [pair] * far + [block_sum] * shards_n
        outs = pl.pallas_call(
            functools.partial(chunk_kernel, devs, held, chunk),
            out_shape=outs,
            grid=(1,),
            in_specs=[SMEM, whole(*depth_filter.shape)]
            + [whole(ROWS, width)] * 2
            + [whole(*value.shape) for value in (*arrived[chunk][2:], *full)],
            out_specs=[whole(*value.shape) for value in outs],
            scratch_shapes=[
                pltpu.VMEM((CHUNK, channels, out_channels), BF16),
                pltpu.VMEM((total, width), F32),
                pltpu.VMEM((bins * block, channels), BF16),
                pltpu.VMEM((bins * block, out_channels), F32),
                pltpu.VMEM((bins * block, out_channels), BF16),
                pltpu.VMEM((bins * block, channels), F32),
                pltpu.VMEM((channels, out_channels), BF16),
                pltpu.VMEM((total, width), BF16),
            ],
            compiler_params=params(),
            cost_estimate=cost(COSTS[1]),
            name="experts",
        )(me_dp, depth_filter, *arrived[chunk], *full)
        results, to_reduce = list(outs[:far]), outs[far:]
        steps[f"sums{chunk}"] = [
            flip(to_reduce[r], "dp", r) for r in sorted(range(1, shards_n), reverse=True)
        ]
        summed = to_reduce[0].astype(F32)
        for value in steps[f"sums{chunk}"]:
            summed = summed + value.astype(F32)
        for expert in range(CHUNK):
            lanes = slice(expert * channels, (expert + 1) * channels)
            taps = summed[CHUNK * local : CHUNK * local + KERNEL_TAPS, lanes]
            reduced.append((summed[expert * local : (expert + 1) * local], taps))
        results = [wait(value, R_AFTER[chunk]) for value in results]
        results[order[-1]] = wait(results[order[-1]], R_LAST[chunk])
        near = along_line(results)
        backs.append(near)
    point_grads = jnp.stack([value for value, _ in reduced], axis=1)
    depth_grads = jnp.stack([value for _, value in reduced], axis=0)
    lists, backs = backs, []
    for chunk, near in enumerate(lists):
        value = jnp.concatenate([value[ROWS:] for value in near], axis=0)
        if LATE == 1 and chunk + 1 == chunks:
            value, point_grads, depth_grads = lax.optimization_barrier(
                (value, point_grads, depth_grads)
            )
        backs += near + [flip(value, "expert", 1)]
    if LATE == 2:
        backs[-1], point_grads, depth_grads = lax.optimization_barrier(
            (backs[-1], point_grads, depth_grads)
        )

    mixed, token_grads = pl.pallas_call(
        functools.partial(combine_kernel, chunks),
        grid=(1,),
        out_shape=[jax.ShapeDtypeStruct((toks, width), BF16)] * 2,
        in_specs=[whole(2, toks)]
        + [whole(3 * toks, total)] * chunks
        + ([whole(ROWS, width)] * far + [whole(far * ROWS, width)]) * chunks,
        out_specs=[whole(toks, width)] * 2,
        compiler_params=params(),
        cost_estimate=cost(COSTS[2]),
        name="combine",
    )(route_weights, *tables, *backs)
    return (mixed, token_grads, point_grads, depth_grads)


def solution(mesh):
    placed = (
        P(("dp", "expert"), None),
        P(("dp", "expert"), None),
        P(("dp", "expert"), None),
        P(("dp", "expert"), None),
        P("expert", None, None),
        P("dp", "expert", None),
    )
    return jax.shard_map(
        shards,
        mesh=mesh,
        in_specs=placed,
        out_specs=(
            P(("dp", "expert"), None),
            P(("dp", "expert"), None),
            P("dp", "expert", None),
            P("expert", None, None),
        ),
        check_vma=False,
    )
```

```python
import functools

import jax
import jax.numpy as jnp
from jax import lax
from jax.experimental import pallas as pl
from jax.experimental.pallas import tpu as pltpu
from jax.sharding import PartitionSpec as P

KERNEL_TAPS = 5
DILATION_STEP = 2
CAP = 4
CHUNK = 2
ROWS = 2 * CHUNK * CAP
PAD = 8
OFFSETS = tuple(DILATION_STEP * (j - KERNEL_TAPS // 2) for j in range(KERNEL_TAPS))
F32 = jnp.float32
BF16 = jnp.bfloat16


def params():
    return pltpu.CompilerParams(vmem_limit_bytes=56 * 1024 * 1024)


def dot(a, b, dims=((1,), (0,))):
    return lax.dot_general(a, b, (dims, ((), ())), preferred_element_type=F32)


def column(row):
    size = row.shape[1]
    diagonal = lax.broadcasted_iota(jnp.int32, (size, size), 0) == lax.broadcasted_iota(
        jnp.int32, (size, size), 1
    )
    return jnp.sum(jnp.where(diagonal, row, jnp.zeros_like(row)), axis=1, keepdims=True)


def dispatch_kernel(devs, chunks, chunk, me_ref, routes_ref, weights_ref, tokens_ref, grads_ref, *refs):
    table_ref, pieces, select_ref = refs[0], refs[1:-1], refs[-1]
    toks, width = tokens_ref.shape
    slots = devs * ROWS
    experts = devs * chunks * CHUNK

    @pl.when(pl.program_id(0) == 0)
    def _():
        me = me_ref[0]
        first = column(routes_ref[0:1, :])
        second = column(routes_ref[1:2, :])
        lane_expert = lax.broadcasted_iota(jnp.int32, (toks, experts), 1)
        hit_first = (first == lane_expert).astype(F32)
        hit_second = (second == lane_expert).astype(F32)
        earlier = (
            lax.broadcasted_iota(jnp.int32, (toks, toks), 1)
            < lax.broadcasted_iota(jnp.int32, (toks, toks), 0)
        ).astype(BF16)
        counts = dot(earlier, (hit_first + hit_second).astype(BF16))
        rank_first = jnp.sum(counts * hit_first, axis=1, keepdims=True).astype(jnp.int32)
        rank_second = jnp.sum(counts * hit_second, axis=1, keepdims=True).astype(jnp.int32)
        slot_first = first * CAP + rank_first
        slot_second = second * CAP + rank_second
        lane = lax.broadcasted_iota(jnp.int32, (1, slots), 1)
        piece = lane // ROWS
        within = lane % ROWS
        relative = piece
        is_frame = within // (CHUNK * CAP) == 0
        wanted = ((me ^ relative) * chunks + chunk) * (CHUNK * CAP) + within % (CHUNK * CAP)
        one = lambda mask: jnp.where(mask, 1.0, 0.0).astype(BF16)
        frame_wanted = jnp.where(is_frame, wanted, -1)
        cotan_wanted = jnp.where(is_frame, -1, wanted)
        frame_first = one(slot_first == frame_wanted)
        frame_second = one(slot_second == frame_wanted)
        cotan_first = one(slot_first == cotan_wanted)
        cotan_second = one(slot_second == cotan_wanted)
        table_ref[0:toks] = frame_first
        table_ref[toks : 2 * toks] = frame_second
        table_ref[2 * toks : 3 * toks] = cotan_first + cotan_second
        select = jnp.concatenate([frame_first + frame_second, cotan_first, cotan_second], axis=0)
        select_ref[...] = select.astype(F32).T.astype(BF16)

    weight_first = column(weights_ref[0:1, :])
    weight_second = column(weights_ref[1:2, :])
    step = min(512, width)
    for begin in range(0, width, step):
        lanes = slice(begin, begin + step)
        grads = grads_ref[:, lanes].astype(F32)
        stacked = jnp.concatenate(
            [
                tokens_ref[:, lanes],
                (weight_first * grads).astype(BF16),
                (weight_second * grads).astype(BF16),
            ],
            axis=0,
        )
        placed = dot(select_ref[...], stacked)
        if chunk < NEAR_SWAPS:
            for r, ref in enumerate(pieces):
                ref[:, lanes] = placed[2 * r * ROWS : 2 * (r + 1) * ROWS].astype(BF16)
        else:
            for r, ref in enumerate(pieces[:-1]):
                begin_row = 2 * r * ROWS
                ref[:, lanes] = placed[begin_row : begin_row + ROWS].astype(BF16)
                pieces[-1][r * ROWS : (r + 1) * ROWS, lanes] = placed[
                    begin_row + ROWS : begin_row + 2 * ROWS
                ].astype(BF16)


def sorting(devs, side):
    total = devs * ROWS
    block = devs * CAP
    row = lax.broadcasted_iota(jnp.int32, (total, total), side)
    expert = row // (2 * block)
    tensor = (row // block) % 2
    device = (row // CAP) % devs
    source = device * ROWS + (tensor * CHUNK + expert) * CAP + row % CAP
    other = lax.broadcasted_iota(jnp.int32, (total, total), 1 - side)
    return jnp.where(source == other, 1.0, 0.0).astype(BF16)


def bits_of(size, expert):
    bits = [1 << k for k in range(size.bit_length() - 1)]
    return bits if expert % 2 == 0 else bits[::-1]


def chunk_kernel(devs, held, chunk, parts, *refs):
    me_ref, filter_ref = refs[0], refs[1]
    refs = refs[2:]
    far = devs // 2
    pieces, refs = refs[: far + 1], refs[far + 1 :]
    weight_refs, refs = refs[: len(held)], refs[len(held) :]
    backs, refs = refs[:far], refs[far:]
    shards_n = sum(map(len, held)) // CHUNK
    reduce_refs, refs = refs[:shards_n], refs[shards_n:]
    matrix, rows_f32, hidden, preact, dpre, dhidden, grad, results = refs
    width = pieces[0].shape[1]
    channels = matrix.shape[1]
    bins = width // channels
    block = devs * CAP
    total = devs * ROWS
    local = channels // shards_n
    for ref, blocks in zip(weight_refs, held):
        for index, (expert, place, relative) in enumerate(blocks):
            begin = pl.multiple_of((me_ref[0] ^ place if relative else place) * local, local)
            matrix[expert, pl.ds(begin, local), :] = ref[index * local : (index + 1) * local]

    sort = sorting(devs, 0)
    for p in range(bins):
        lanes = slice(p * channels, (p + 1) * channels)
        stacked = [pieces[i][begin : begin + rows, lanes] for i, begin, rows in parts]
        rows_f32[:, lanes] = dot(sort, jnp.concatenate(stacked, axis=0))

    for expert in range(CHUNK):
        frames = slice(expert * 2 * block, expert * 2 * block + block)
        cotans = slice(expert * 2 * block + block, (expert + 1) * 2 * block)
        taps = [filter_ref[chunk * CHUNK + expert, j : j + 1, :] for j in range(KERNEL_TAPS)]
        bin_lanes = lambda p: slice(p * channels, (p + 1) * channels)
        bin_rows = lambda p: slice(p * block, (p + 1) * block)
        for p in range(bins):
            acc = None
            for j, off in enumerate(OFFSETS):
                if 0 <= p + off < bins:
                    term = taps[j] * rows_f32[frames, bin_lanes(p + off)]
                    acc = term if acc is None else acc + term
            hidden[bin_rows(p), :] = acc.astype(BF16)
        preact[...] = dot(hidden[...], matrix[expert])
        for p in range(bins):
            value = preact[bin_rows(p), 0:channels]
            sig = 1.0 / (1.0 + jnp.exp(-preact[bin_rows(p), channels : 2 * channels]))
            cotan = rows_f32[cotans, bin_lanes(p)]
            results[frames, bin_lanes(p)] = (value * sig).astype(BF16)
            dpre[bin_rows(p), 0:channels] = (cotan * sig).astype(BF16)
            dpre[bin_rows(p), channels : 2 * channels] = (
                cotan * value * sig * (1.0 - sig)
            ).astype(BF16)
        dhidden[...] = dot(dpre[...], matrix[expert], ((1,), (1,)))
        grad[...] = dot(hidden[...], dpre[...], ((0,), (0,))).astype(BF16)
        for relative, ref in enumerate(reduce_refs):
            begin = pl.multiple_of((me_ref[0] ^ relative) * local, local)
            ref[expert * local : (expert + 1) * local, :] = grad[pl.ds(begin, local), :]
        for q in range(bins):
            acc = None
            for j, off in enumerate(OFFSETS):
                if 0 <= q - off < bins:
                    term = taps[j] * dhidden[bin_rows(q - off), :]
                    acc = term if acc is None else acc + term
            results[cotans, bin_lanes(q)] = acc.astype(BF16)
        lines = []
        for j, off in enumerate(OFFSETS):
            acc = None
            for p in range(bins):
                if 0 <= p + off < bins:
                    term = dhidden[bin_rows(p), :] * rows_f32[frames, bin_lanes(p + off)]
                    acc = term if acc is None else acc + term
            lines.append(jnp.sum(acc, axis=0, keepdims=True))
        tail = jnp.concatenate(lines + [jnp.zeros((PAD - KERNEL_TAPS, channels), F32)], axis=0)
        lanes = slice(expert * channels, (expert + 1) * channels)
        for ref in reduce_refs:
            ref[CHUNK * local : CHUNK * local + PAD, lanes] = tail.astype(BF16)
    unsort = sorting(devs, 1)
    for p in range(bins):
        lanes = slice(p * channels, (p + 1) * channels)
        placed = dot(unsort, results[:, lanes])
        for r, ref in enumerate(backs):
            ref[:, lanes] = placed[2 * r * ROWS : 2 * (r + 1) * ROWS].astype(BF16)


def combine_kernel(chunks, weights_ref, *refs):
    tables, pieces, (mixed_ref, grads_ref) = refs[:chunks], refs[chunks:-2], refs[-2:]
    each = len(pieces) // chunks
    table = jnp.concatenate([ref[...] for ref in tables], axis=1)
    toks, width = mixed_ref.shape
    weight_first = column(weights_ref[0:1, :])
    weight_second = column(weights_ref[1:2, :])
    step = min(512, width)
    for begin in range(0, width, step):
        lanes = slice(begin, begin + step)
        stacked = []
        for index in range(chunks):
            *near, swapped = pieces[index * each : (index + 1) * each]
            for r, ref in enumerate(near):
                stacked += [ref[:, lanes], swapped[r * ROWS : (r + 1) * ROWS, lanes]]
        placed = dot(table, jnp.concatenate(stacked, axis=0))
        mixed_ref[:, lanes] = (
            weight_first * placed[0:toks] + weight_second * placed[toks : 2 * toks]
        ).astype(BF16)
        grads_ref[:, lanes] = placed[2 * toks : 3 * toks].astype(BF16)


VMEM = pl.BlockSpec(memory_space=pltpu.VMEM)
SMEM = pl.BlockSpec(memory_space=pltpu.SMEM)
COSTS = (2, 3, 2)
LATE = 1
PLANE = 2
GATHER_AFTER = False
NEAR_SWAPS = 1
ORDER = lambda s: -s
SUMS_AFTER = False
WEIGHTS_AFTER = 0
SWAP_AFTER = 2
D1_AFTER = "gather0last"
K_AFTER = ["gather1first", ""]
R_AFTER = ['gather1last', 'sums0']
R_LAST = ["", ""]
WINDOW = 3


def cost(work):
    return pl.CostEstimate(flops=work * 10**9, transcendentals=0, bytes_accessed=8 * 1024 * 1024)


def flip(value, axis, bits):
    return lax.ppermute(value, axis, [(k, k ^ bits) for k in range(lax.axis_size(axis))])


def after(value, *others):
    return lax.optimization_barrier((value, *others))[0]


def shards(tokens, grads_out, routes, route_weights, depth_filter, point_weight):
    toks, width = tokens.shape
    devs = lax.axis_size("expert")
    shards_n = lax.axis_size("dp")
    exp_local = depth_filter.shape[0]
    chunks = exp_local // CHUNK
    local, _, out_channels = point_weight.shape
    channels = local * shards_n
    bins = width // channels
    block = devs * CAP
    total = devs * ROWS
    far = devs // 2
    order = sorted(range(1, far), key=ORDER)
    me = lax.axis_index("expert").astype(jnp.int32).reshape(1)
    me_dp = lax.axis_index("dp").astype(jnp.int32).reshape(1)
    routes = routes.T
    route_weights = route_weights.T

    whole = lambda *shape: pl.BlockSpec(shape, lambda i: (0,) * len(shape))
    piece = jax.ShapeDtypeStruct((ROWS, width), BF16)
    tables, sent = [], []
    pair = jax.ShapeDtypeStruct((2 * ROWS, width), BF16)
    for chunk in range(chunks):
        if chunk < NEAR_SWAPS:
            shapes = [pair] * far
        else:
            shapes = [piece] * far + [jax.ShapeDtypeStruct((far * ROWS, width), BF16)]
        table, *pieces = pl.pallas_call(
            functools.partial(dispatch_kernel, devs, chunks, chunk),
            grid=(1,),
            out_shape=[jax.ShapeDtypeStruct((3 * toks, total), BF16)] + shapes,
            in_specs=[SMEM, whole(2, toks), whole(2, toks), whole(toks, width), whole(toks, width)],
            out_specs=[whole(3 * toks, total)] + [whole(*value.shape) for value in shapes],
            scratch_shapes=[pltpu.VMEM((total, 3 * toks), BF16)],
            compiler_params=params(),
            cost_estimate=cost(COSTS[0]),
            name="dispatch",
        )(me, routes, route_weights, tokens, grads_out)
        tables.append(table)
        sent.append(pieces)

    line = []

    def along_line(pieces):
        moved = {0: pieces[0]}
        for r in order:
            value = pieces[r]
            if len(line) >= WINDOW:
                value = after(value, line[-WINDOW])
            line.append(flip(value, "expert", 2 * r))
            moved[r] = line[-1]
        return [moved[r] for r in range(far)]

    plane = []
    steps = {}
    rounds_n = shards_n.bit_length() - 1

    def in_plane(value, bit, step):
        if len(plane) >= PLANE:
            value = after(value, plane[-PLANE])
        plane.append(flip(value, "dp", bit))
        steps.setdefault(step, []).append(plane[-1])
        return plane[-1]

    def wait(value, name):
        names = [n for n in (name or "").split() if n]
        others = [v for n in names for v in steps[n]]
        return after(value, *others) if others else value

    def gather(parts, chunk):
        held = [(part, [0]) for part in parts]
        for turn in range(shards_n.bit_length() - 1):
            bits = [bits_of(shards_n, expert)[turn] for expert in range(CHUNK)]
            step = f"gather{chunk}" + ("first" if turn == 0 else "last")
            came = [in_plane(value, bit, step) for (value, _), bit in zip(held, bits)]
            new = [
                (other, [place ^ bit for place in places])
                for (_, places), other, bit in zip(held, came, bits)
            ]
            if 2 * len(held[0][1]) == shards_n:
                return [
                    (value, [(expert, place, True) for place in places])
                    for expert in range(CHUNK)
                    for value, places in (held[expert], new[expert])
                ]
            held = [
                (jnp.concatenate([old, other], axis=0), places + more)
                for (old, places), (other, more) in zip(held, new)
            ]

    weights = jnp.transpose(after(point_weight, tables[WEIGHTS_AFTER]), (1, 0, 2))
    def dispatched(chunk):
        if chunk < NEAR_SWAPS:
            near = [sent[chunk][0]] + [
                wait(value, D1_AFTER) if chunk > 0 else value for value in sent[chunk][1:]
            ]
            near = along_line(near)
            value = jnp.concatenate([value[ROWS:] for value in near], axis=0)
            parts = [p for r in range(far) for p in ((r, 0, ROWS), (far, r * ROWS, ROWS))]
            return near + [flip(value, "expert", 1)], parts
        *own, relayed = sent[chunk]
        if SWAP_AFTER is not None:
            relayed = after(relayed, line[SWAP_AFTER])
        relayed = flip(relayed, "expert", 1)
        pairs = [
            jnp.concatenate([own[r], relayed[r * ROWS : (r + 1) * ROWS]], axis=0)
            for r in range(1, far)
        ]
        if chunk > 0:
            pairs = [wait(value, D1_AFTER) for value in pairs]
        parts = [(0, 0, ROWS), (1, 0, ROWS)] + [(r + 1, 0, 2 * ROWS) for r in range(1, far)]
        return [own[0], relayed] + along_line([own[0]] + pairs)[1:], parts

    def weights_of(chunk, other):
        parts = [weights[chunk * CHUNK + expert] for expert in range(CHUNK)]
        return gather(parts if other is False else [after(part, other) for part in parts], chunk)

    arrived = [dispatched(0)]
    gathered = [weights_of(0, GATHER_AFTER and flip(sent[1][-1], "expert", 1))]
    for chunk in range(1, chunks):
        gathered.append(weights_of(chunk, sent[chunk][-1]))
        arrived.append(dispatched(chunk))
    block_sum = jax.ShapeDtypeStruct((CHUNK * local + PAD, out_channels), BF16)
    backs = []
    reduced = []
    for chunk in range(chunks):
        full, held = zip(*gathered[chunk])
        came, parts = arrived[chunk]
        came[0] = wait(came[0], K_AFTER[chunk])
        outs = [pair] * far + [block_sum] * shards_n
        outs = pl.pallas_call(
            functools.partial(chunk_kernel, devs, held, chunk, parts),
            out_shape=outs,
            grid=(1,),
            in_specs=[SMEM, whole(*depth_filter.shape)]
            + [
                whole(max(begin + n for i, begin, n in parts if i == index), width)
                for index in range(len(came))
            ]
            + [whole(*value.shape) for value in full],
            out_specs=[whole(*value.shape) for value in outs],
            scratch_shapes=[
                pltpu.VMEM((CHUNK, channels, out_channels), BF16),
                pltpu.VMEM((total, width), F32),
                pltpu.VMEM((bins * block, channels), BF16),
                pltpu.VMEM((bins * block, out_channels), F32),
                pltpu.VMEM((bins * block, out_channels), BF16),
                pltpu.VMEM((bins * block, channels), F32),
                pltpu.VMEM((channels, out_channels), BF16),
                pltpu.VMEM((total, width), BF16),
            ],
            compiler_params=params(),
            cost_estimate=cost(COSTS[1]),
            name="experts",
        )(me_dp, depth_filter, *came, *full)
        results, to_reduce = list(outs[:far]), outs[far:]
        if chunk + 1 < chunks and SUMS_AFTER:
            to_reduce = [after(value, arrived[chunk + 1][0][-1]) for value in to_reduce]
        steps[f"sums{chunk}"] = [
            flip(to_reduce[r], "dp", r) for r in sorted(range(1, shards_n), reverse=True)
        ]
        summed = to_reduce[0].astype(F32)
        for value in steps[f"sums{chunk}"]:
            summed = summed + value.astype(F32)
        for expert in range(CHUNK):
            lanes = slice(expert * channels, (expert + 1) * channels)
            taps = summed[CHUNK * local : CHUNK * local + KERNEL_TAPS, lanes]
            reduced.append((summed[expert * local : (expert + 1) * local], taps))
        results = [wait(value, R_AFTER[chunk]) for value in results]
        results[order[-1]] = wait(results[order[-1]], R_LAST[chunk])
        near = along_line(results)
        backs.append(near)
    point_grads = jnp.stack([value for value, _ in reduced], axis=1)
    depth_grads = jnp.stack([value for _, value in reduced], axis=0)
    lists, backs = backs, []
    for chunk, near in enumerate(lists):
        value = jnp.concatenate([value[ROWS:] for value in near], axis=0)
        if LATE == 1 and chunk + 1 == chunks:
            value, point_grads, depth_grads = lax.optimization_barrier(
                (value, point_grads, depth_grads)
            )
        backs += near + [flip(value, "expert", 1)]
    if LATE == 2:
        backs[-1], point_grads, depth_grads = lax.optimization_barrier(
            (backs[-1], point_grads, depth_grads)
        )

    mixed, token_grads = pl.pallas_call(
        functools.partial(combine_kernel, chunks),
        grid=(1,),
        out_shape=[jax.ShapeDtypeStruct((toks, width), BF16)] * 2,
        in_specs=[whole(2, toks)]
        + [whole(3 * toks, total)] * chunks
        + ([whole(ROWS, width)] * far + [whole(far * ROWS, width)]) * chunks,
        out_specs=[whole(toks, width)] * 2,
        compiler_params=params(),
        cost_estimate=cost(COSTS[2]),
        name="combine",
    )(route_weights, *tables, *backs)
    return (mixed, token_grads, point_grads, depth_grads)


def solution(mesh):
    placed = (
        P(("dp", "expert"), None),
        P(("dp", "expert"), None),
        P(("dp", "expert"), None),
        P(("dp", "expert"), None),
        P("expert", None, None),
        P("dp", "expert", None),
    )
    return jax.shard_map(
        shards,
        mesh=mesh,
        in_specs=placed,
        out_specs=(
            P(("dp", "expert"), None),
            P(("dp", "expert"), None),
            P("dp", "expert", None),
            P("expert", None, None),
        ),
        check_vma=False,
    )
```

```python
import functools

import jax
import jax.numpy as jnp
from jax import lax
from jax.experimental import pallas as pl
from jax.experimental.pallas import tpu as pltpu
from jax.sharding import PartitionSpec as P

KERNEL_TAPS = 5
DILATION_STEP = 2
CAP = 4
CHUNK = 2
ROWS = 2 * CHUNK * CAP
PAD = 8
OFFSETS = tuple(DILATION_STEP * (j - KERNEL_TAPS // 2) for j in range(KERNEL_TAPS))
F32 = jnp.float32
BF16 = jnp.bfloat16


def params():
    return pltpu.CompilerParams(vmem_limit_bytes=56 * 1024 * 1024)


def dot(a, b, dims=((1,), (0,))):
    return lax.dot_general(a, b, (dims, ((), ())), preferred_element_type=F32)


def column(row):
    size = row.shape[1]
    diagonal = lax.broadcasted_iota(jnp.int32, (size, size), 0) == lax.broadcasted_iota(
        jnp.int32, (size, size), 1
    )
    return jnp.sum(jnp.where(diagonal, row, jnp.zeros_like(row)), axis=1, keepdims=True)


def dispatch_kernel(devs, chunks, chunk, me_ref, routes_ref, weights_ref, tokens_ref, grads_ref, *refs):
    table_ref, pieces, select_ref = refs[0], refs[1:-1], refs[-1]
    toks, width = tokens_ref.shape
    slots = devs * ROWS
    experts = devs * chunks * CHUNK

    @pl.when(pl.program_id(0) == 0)
    def _():
        me = me_ref[0]
        first = column(routes_ref[0:1, :])
        second = column(routes_ref[1:2, :])
        lane_expert = lax.broadcasted_iota(jnp.int32, (toks, experts), 1)
        hit_first = (first == lane_expert).astype(F32)
        hit_second = (second == lane_expert).astype(F32)
        earlier = (
            lax.broadcasted_iota(jnp.int32, (toks, toks), 1)
            < lax.broadcasted_iota(jnp.int32, (toks, toks), 0)
        ).astype(BF16)
        counts = dot(earlier, (hit_first + hit_second).astype(BF16))
        rank_first = jnp.sum(counts * hit_first, axis=1, keepdims=True).astype(jnp.int32)
        rank_second = jnp.sum(counts * hit_second, axis=1, keepdims=True).astype(jnp.int32)
        slot_first = first * CAP + rank_first
        slot_second = second * CAP + rank_second
        lane = lax.broadcasted_iota(jnp.int32, (1, slots), 1)
        piece = lane // ROWS
        within = lane % ROWS
        relative = piece
        is_frame = within // (CHUNK * CAP) == 0
        wanted = ((me ^ relative) * chunks + chunk) * (CHUNK * CAP) + within % (CHUNK * CAP)
        one = lambda mask: jnp.where(mask, 1.0, 0.0).astype(BF16)
        frame_wanted = jnp.where(is_frame, wanted, -1)
        cotan_wanted = jnp.where(is_frame, -1, wanted)
        frame_first = one(slot_first == frame_wanted)
        frame_second = one(slot_second == frame_wanted)
        cotan_first = one(slot_first == cotan_wanted)
        cotan_second = one(slot_second == cotan_wanted)
        table_ref[0:toks] = frame_first
        table_ref[toks : 2 * toks] = frame_second
        table_ref[2 * toks : 3 * toks] = cotan_first + cotan_second
        select = jnp.concatenate([frame_first + frame_second, cotan_first, cotan_second], axis=0)
        select_ref[...] = select.astype(F32).T.astype(BF16)

    weight_first = column(weights_ref[0:1, :])
    weight_second = column(weights_ref[1:2, :])
    step = min(512, width)
    for begin in range(0, width, step):
        lanes = slice(begin, begin + step)
        grads = grads_ref[:, lanes].astype(F32)
        stacked = jnp.concatenate(
            [
                tokens_ref[:, lanes],
                (weight_first * grads).astype(BF16),
                (weight_second * grads).astype(BF16),
            ],
            axis=0,
        )
        placed = dot(select_ref[...], stacked)
        if chunk < NEAR_SWAPS:
            for r, ref in enumerate(pieces):
                ref[:, lanes] = placed[2 * r * ROWS : 2 * (r + 1) * ROWS].astype(BF16)
        else:
            for r, ref in enumerate(pieces[:-1]):
                begin_row = 2 * r * ROWS
                ref[:, lanes] = placed[begin_row : begin_row + ROWS].astype(BF16)
                pieces[-1][r * ROWS : (r + 1) * ROWS, lanes] = placed[
                    begin_row + ROWS : begin_row + 2 * ROWS
                ].astype(BF16)


def sorting(devs, side):
    total = devs * ROWS
    block = devs * CAP
    row = lax.broadcasted_iota(jnp.int32, (total, total), side)
    expert = row // (2 * block)
    tensor = (row // block) % 2
    device = (row // CAP) % devs
    source = device * ROWS + (tensor * CHUNK + expert) * CAP + row % CAP
    other = lax.broadcasted_iota(jnp.int32, (total, total), 1 - side)
    return jnp.where(source == other, 1.0, 0.0).astype(BF16)


def bits_of(size, expert):
    bits = [1 << k for k in range(size.bit_length() - 1)]
    return bits if expert % 2 == 0 else bits[::-1]


def chunk_kernel(devs, held, chunk, parts, *refs):
    me_ref, filter_ref = refs[0], refs[1]
    refs = refs[2:]
    far = devs // 2
    pieces, refs = refs[: far + 1], refs[far + 1 :]
    weight_refs, refs = refs[: len(held)], refs[len(held) :]
    backs, refs = refs[:far], refs[far:]
    shards_n = sum(map(len, held)) // CHUNK
    reduce_refs, refs = refs[:shards_n], refs[shards_n:]
    matrix, rows_f32, hidden, preact, dpre, dhidden, grad, results = refs
    width = pieces[0].shape[1]
    channels = matrix.shape[1]
    bins = width // channels
    block = devs * CAP
    total = devs * ROWS
    local = channels // shards_n
    for ref, blocks in zip(weight_refs, held):
        for index, (expert, place, relative) in enumerate(blocks):
            begin = pl.multiple_of((me_ref[0] ^ place if relative else place) * local, local)
            matrix[expert, pl.ds(begin, local), :] = ref[index * local : (index + 1) * local]

    sort = sorting(devs, 0)
    for p in range(bins):
        lanes = slice(p * channels, (p + 1) * channels)
        stacked = [pieces[i][begin : begin + rows, lanes] for i, begin, rows in parts]
        rows_f32[:, lanes] = dot(sort, jnp.concatenate(stacked, axis=0))

    for expert in range(CHUNK):
        frames = slice(expert * 2 * block, expert * 2 * block + block)
        cotans = slice(expert * 2 * block + block, (expert + 1) * 2 * block)
        taps = [filter_ref[chunk * CHUNK + expert, j : j + 1, :] for j in range(KERNEL_TAPS)]
        bin_lanes = lambda p: slice(p * channels, (p + 1) * channels)
        bin_rows = lambda p: slice(p * block, (p + 1) * block)
        for p in range(bins):
            acc = None
            for j, off in enumerate(OFFSETS):
                if 0 <= p + off < bins:
                    term = taps[j] * rows_f32[frames, bin_lanes(p + off)]
                    acc = term if acc is None else acc + term
            hidden[bin_rows(p), :] = acc.astype(BF16)
        preact[...] = dot(hidden[...], matrix[expert])
        for p in range(bins):
            value = preact[bin_rows(p), 0:channels]
            sig = 1.0 / (1.0 + jnp.exp(-preact[bin_rows(p), channels : 2 * channels]))
            cotan = rows_f32[cotans, bin_lanes(p)]
            results[frames, bin_lanes(p)] = (value * sig).astype(BF16)
            dpre[bin_rows(p), 0:channels] = (cotan * sig).astype(BF16)
            dpre[bin_rows(p), channels : 2 * channels] = (
                cotan * value * sig * (1.0 - sig)
            ).astype(BF16)
        dhidden[...] = dot(dpre[...], matrix[expert], ((1,), (1,)))
        grad[...] = dot(hidden[...], dpre[...], ((0,), (0,))).astype(BF16)
        for relative, ref in enumerate(reduce_refs):
            begin = pl.multiple_of((me_ref[0] ^ relative) * local, local)
            ref[expert * local : (expert + 1) * local, :] = grad[pl.ds(begin, local), :]
        for q in range(bins):
            acc = None
            for j, off in enumerate(OFFSETS):
                if 0 <= q - off < bins:
                    term = taps[j] * dhidden[bin_rows(q - off), :]
                    acc = term if acc is None else acc + term
            results[cotans, bin_lanes(q)] = acc.astype(BF16)
        lines = []
        for j, off in enumerate(OFFSETS):
            acc = None
            for p in range(bins):
                if 0 <= p + off < bins:
                    term = dhidden[bin_rows(p), :] * rows_f32[frames, bin_lanes(p + off)]
                    acc = term if acc is None else acc + term
            lines.append(jnp.sum(acc, axis=0, keepdims=True))
        tail = jnp.concatenate(lines + [jnp.zeros((PAD - KERNEL_TAPS, channels), F32)], axis=0)
        lanes = slice(expert * channels, (expert + 1) * channels)
        for ref in reduce_refs:
            ref[CHUNK * local : CHUNK * local + PAD, lanes] = tail.astype(BF16)
    unsort = sorting(devs, 1)
    for p in range(bins):
        lanes = slice(p * channels, (p + 1) * channels)
        placed = dot(unsort, results[:, lanes])
        for r, ref in enumerate(backs):
            ref[:, lanes] = placed[2 * r * ROWS : 2 * (r + 1) * ROWS].astype(BF16)


def combine_kernel(chunks, weights_ref, *refs):
    tables, pieces, (mixed_ref, grads_ref) = refs[:chunks], refs[chunks:-2], refs[-2:]
    each = len(pieces) // chunks
    table = jnp.concatenate([ref[...] for ref in tables], axis=1)
    toks, width = mixed_ref.shape
    weight_first = column(weights_ref[0:1, :])
    weight_second = column(weights_ref[1:2, :])
    step = min(512, width)
    for begin in range(0, width, step):
        lanes = slice(begin, begin + step)
        stacked = []
        for index in range(chunks):
            *near, swapped = pieces[index * each : (index + 1) * each]
            for r, ref in enumerate(near):
                stacked += [ref[:, lanes], swapped[r * ROWS : (r + 1) * ROWS, lanes]]
        placed = dot(table, jnp.concatenate(stacked, axis=0))
        mixed_ref[:, lanes] = (
            weight_first * placed[0:toks] + weight_second * placed[toks : 2 * toks]
        ).astype(BF16)
        grads_ref[:, lanes] = placed[2 * toks : 3 * toks].astype(BF16)


VMEM = pl.BlockSpec(memory_space=pltpu.VMEM)
SMEM = pl.BlockSpec(memory_space=pltpu.SMEM)
COSTS = (2, 8, 2)
LATE = 1
PLANE = 2
GATHER_AFTER = False
NEAR_SWAPS = 1
ORDER = lambda s: -s
SUMS_AFTER = False
WEIGHTS_AFTER = 0
SWAP_AFTER = 2
D1_AFTER = "gather0last"
K_AFTER = ["gather1first", ""]
R_AFTER = ['gather1last', 'sums0']
R_LAST = ["", ""]
WINDOW = 3


def cost(work):
    return pl.CostEstimate(flops=work * 10**9, transcendentals=0, bytes_accessed=8 * 1024 * 1024)


def flip(value, axis, bits):
    return lax.ppermute(value, axis, [(k, k ^ bits) for k in range(lax.axis_size(axis))])


def after(value, *others):
    return lax.optimization_barrier((value, *others))[0]


def shards(tokens, grads_out, routes, route_weights, depth_filter, point_weight):
    toks, width = tokens.shape
    devs = lax.axis_size("expert")
    shards_n = lax.axis_size("dp")
    exp_local = depth_filter.shape[0]
    chunks = exp_local // CHUNK
    local, _, out_channels = point_weight.shape
    channels = local * shards_n
    bins = width // channels
    block = devs * CAP
    total = devs * ROWS
    far = devs // 2
    order = sorted(range(1, far), key=ORDER)
    me = lax.axis_index("expert").astype(jnp.int32).reshape(1)
    me_dp = lax.axis_index("dp").astype(jnp.int32).reshape(1)
    routes = routes.T
    route_weights = route_weights.T

    whole = lambda *shape: pl.BlockSpec(shape, lambda i: (0,) * len(shape))
    piece = jax.ShapeDtypeStruct((ROWS, width), BF16)
    tables, sent = [], []
    pair = jax.ShapeDtypeStruct((2 * ROWS, width), BF16)
    for chunk in range(chunks):
        if chunk < NEAR_SWAPS:
            shapes = [pair] * far
        else:
            shapes = [piece] * far + [jax.ShapeDtypeStruct((far * ROWS, width), BF16)]
        table, *pieces = pl.pallas_call(
            functools.partial(dispatch_kernel, devs, chunks, chunk),
            grid=(1,),
            out_shape=[jax.ShapeDtypeStruct((3 * toks, total), BF16)] + shapes,
            in_specs=[SMEM, whole(2, toks), whole(2, toks), whole(toks, width), whole(toks, width)],
            out_specs=[whole(3 * toks, total)] + [whole(*value.shape) for value in shapes],
            scratch_shapes=[pltpu.VMEM((total, 3 * toks), BF16)],
            compiler_params=params(),
            cost_estimate=cost(COSTS[0]),
            name="dispatch",
        )(me, routes, route_weights, tokens, grads_out)
        tables.append(table)
        sent.append(pieces)

    line = []

    def along_line(pieces):
        moved = {0: pieces[0]}
        for r in order:
            value = pieces[r]
            if len(line) >= WINDOW:
                value = after(value, line[-WINDOW])
            line.append(flip(value, "expert", 2 * r))
            moved[r] = line[-1]
        return [moved[r] for r in range(far)]

    plane = []
    steps = {}
    rounds_n = shards_n.bit_length() - 1

    def in_plane(value, bit, step):
        if len(plane) >= PLANE:
            value = after(value, plane[-PLANE])
        plane.append(flip(value, "dp", bit))
        steps.setdefault(step, []).append(plane[-1])
        return plane[-1]

    def wait(value, name):
        names = [n for n in (name or "").split() if n]
        others = [v for n in names for v in steps[n]]
        return after(value, *others) if others else value

    def gather(parts, chunk):
        held = [(part, [0]) for part in parts]
        for turn in range(shards_n.bit_length() - 1):
            bits = [bits_of(shards_n, expert)[turn] for expert in range(CHUNK)]
            step = f"gather{chunk}" + ("first" if turn == 0 else "last")
            came = [in_plane(value, bit, step) for (value, _), bit in zip(held, bits)]
            new = [
                (other, [place ^ bit for place in places])
                for (_, places), other, bit in zip(held, came, bits)
            ]
            if 2 * len(held[0][1]) == shards_n:
                return [
                    (value, [(expert, place, True) for place in places])
                    for expert in range(CHUNK)
                    for value, places in (held[expert], new[expert])
                ]
            held = [
                (jnp.concatenate([old, other], axis=0), places + more)
                for (old, places), (other, more) in zip(held, new)
            ]

    weights = jnp.transpose(after(point_weight, tables[WEIGHTS_AFTER]), (1, 0, 2))
    def dispatched(chunk):
        if chunk < NEAR_SWAPS:
            near = [sent[chunk][0]] + [
                wait(value, D1_AFTER) if chunk > 0 else value for value in sent[chunk][1:]
            ]
            near = along_line(near)
            value = jnp.concatenate([value[ROWS:] for value in near], axis=0)
            parts = [p for r in range(far) for p in ((r, 0, ROWS), (far, r * ROWS, ROWS))]
            return near + [flip(value, "expert", 1)], parts
        *own, relayed = sent[chunk]
        if SWAP_AFTER is not None:
            relayed = after(relayed, line[SWAP_AFTER])
        relayed = flip(relayed, "expert", 1)
        pairs = [
            jnp.concatenate([own[r], relayed[r * ROWS : (r + 1) * ROWS]], axis=0)
            for r in range(1, far)
        ]
        if chunk > 0:
            pairs = [wait(value, D1_AFTER) for value in pairs]
        parts = [(0, 0, ROWS), (1, 0, ROWS)] + [(r + 1, 0, 2 * ROWS) for r in range(1, far)]
        return [own[0], relayed] + along_line([own[0]] + pairs)[1:], parts

    def weights_of(chunk, other):
        parts = [weights[chunk * CHUNK + expert] for expert in range(CHUNK)]
        return gather(parts if other is False else [after(part, other) for part in parts], chunk)

    arrived = [dispatched(0)]
    gathered = [weights_of(0, GATHER_AFTER and flip(sent[1][-1], "expert", 1))]
    for chunk in range(1, chunks):
        gathered.append(weights_of(chunk, sent[chunk][-1]))
        arrived.append(dispatched(chunk))
    block_sum = jax.ShapeDtypeStruct((CHUNK * local + PAD, out_channels), BF16)
    backs = []
    reduced = []
    for chunk in range(chunks):
        full, held = zip(*gathered[chunk])
        came, parts = arrived[chunk]
        came[0] = wait(came[0], K_AFTER[chunk])
        outs = [pair] * far + [block_sum] * shards_n
        outs = pl.pallas_call(
            functools.partial(chunk_kernel, devs, held, chunk, parts),
            out_shape=outs,
            grid=(1,),
            in_specs=[SMEM, whole(*depth_filter.shape)]
            + [
                whole(max(begin + n for i, begin, n in parts if i == index), width)
                for index in range(len(came))
            ]
            + [whole(*value.shape) for value in full],
            out_specs=[whole(*value.shape) for value in outs],
            scratch_shapes=[
                pltpu.VMEM((CHUNK, channels, out_channels), BF16),
                pltpu.VMEM((total, width), F32),
                pltpu.VMEM((bins * block, channels), BF16),
                pltpu.VMEM((bins * block, out_channels), F32),
                pltpu.VMEM((bins * block, out_channels), BF16),
                pltpu.VMEM((bins * block, channels), F32),
                pltpu.VMEM((channels, out_channels), BF16),
                pltpu.VMEM((total, width), BF16),
            ],
            compiler_params=params(),
            cost_estimate=cost(COSTS[1]),
            name="experts",
        )(me_dp, depth_filter, *came, *full)
        results, to_reduce = list(outs[:far]), outs[far:]
        if chunk + 1 < chunks and SUMS_AFTER:
            to_reduce = [after(value, arrived[chunk + 1][0][-1]) for value in to_reduce]
        steps[f"sums{chunk}"] = [
            flip(to_reduce[r], "dp", r) for r in sorted(range(1, shards_n), reverse=True)
        ]
        summed = to_reduce[0].astype(F32)
        for value in steps[f"sums{chunk}"]:
            summed = summed + value.astype(F32)
        for expert in range(CHUNK):
            lanes = slice(expert * channels, (expert + 1) * channels)
            taps = summed[CHUNK * local : CHUNK * local + KERNEL_TAPS, lanes]
            reduced.append((summed[expert * local : (expert + 1) * local], taps))
        results = [wait(value, R_AFTER[chunk]) for value in results]
        results[order[-1]] = wait(results[order[-1]], R_LAST[chunk])
        near = along_line(results)
        backs.append(near)
    point_grads = jnp.stack([value for value, _ in reduced], axis=1)
    depth_grads = jnp.stack([value for _, value in reduced], axis=0)
    lists, backs = backs, []
    for chunk, near in enumerate(lists):
        value = jnp.concatenate([value[ROWS:] for value in near], axis=0)
        if LATE == 1 and chunk + 1 == chunks:
            value, point_grads, depth_grads = lax.optimization_barrier(
                (value, point_grads, depth_grads)
            )
        backs += near + [flip(value, "expert", 1)]
    if LATE == 2:
        backs[-1], point_grads, depth_grads = lax.optimization_barrier(
            (backs[-1], point_grads, depth_grads)
        )

    mixed, token_grads = pl.pallas_call(
        functools.partial(combine_kernel, chunks),
        grid=(1,),
        out_shape=[jax.ShapeDtypeStruct((toks, width), BF16)] * 2,
        in_specs=[whole(2, toks)]
        + [whole(3 * toks, total)] * chunks
        + ([whole(ROWS, width)] * far + [whole(far * ROWS, width)]) * chunks,
        out_specs=[whole(toks, width)] * 2,
        compiler_params=params(),
        cost_estimate=cost(COSTS[2]),
        name="combine",
    )(route_weights, *tables, *backs)
    return (mixed, token_grads, point_grads, depth_grads)


def solution(mesh):
    placed = (
        P(("dp", "expert"), None),
        P(("dp", "expert"), None),
        P(("dp", "expert"), None),
        P(("dp", "expert"), None),
        P("expert", None, None),
        P("dp", "expert", None),
    )
    return jax.shard_map(
        shards,
        mesh=mesh,
        in_specs=placed,
        out_specs=(
            P(("dp", "expert"), None),
            P(("dp", "expert"), None),
            P("dp", "expert", None),
            P("expert", None, None),
        ),
        check_vma=False,
    )
```
